128 devices in a mesh: seg: 16 (over z, x), col: 8 (over y, core).
Axes of the slice: x: 4, y: 4, z: 4, core: 2. Of those that a mesh axis runs over, the one named last changes fastest.
Arguments:
- margin: float32 [3072, 3072], P('seg'), as said below
- leaf_factor: float32 [3072, 3072], P('seg', 'col'), as said below
Outputs:
- factor: float32 [3072, 3072], P('seg', 'col')
- errors: float32 [2], replicated
Inputs may be any that keep to these rules, and one draw needn't show every extreme that they name: margin is symmetric and positive definite; entries with |row - column| >= 2048 are zero. leaf_factor is zero outside the four diagonal blocks of 768 rows and columns; each block is upper triangular.
All inputs are finite; a program needn't handle non-finite values.
Results may differ from the reference program's by a relative error of at most 0.00005.
Values sent between devices are 32-bit elements; how exact they have to be, the bound alone decides.
No kernel may reach another device: no remote copies, remote signals or barrier semaphores. Data moves between devices by JAX's collectives and lax.ppermute only.
A program may use at most 64 MiB of HBM per device.

```python
import jax
import jax.numpy as jnp
from jax import lax

BAND = 2048
N = 3072


def margin_parts(key):
    base_key = jax.random.fold_in(key, 7)
    entry_key, rough_key, diag_key, noise_key = jax.random.split(base_key, 4)
    indices = jnp.arange(N)
    distance = indices[:, None] - indices[None, :]
    inband = (distance >= 0) & (distance < BAND)
    entries = jax.random.normal(entry_key, (N, N), jnp.float32)
    diagonal = jax.random.uniform(diag_key, (N,), jnp.float32, 0.5, 1.5)
    rough = jax.random.uniform(rough_key, (N,), jnp.float32, 0.7, 1.3)
    rising = 0.6 + 0.6 * indices.astype(jnp.float32) / N
    sigma = 0.5 / jnp.sqrt(jnp.float32(BAND))
    lower = jnp.where(inband, entries, 0.0) * (sigma * rough * rising)[:, None]
    margin = jnp.dot(lower, lower.T, precision=lax.Precision.HIGHEST) + jnp.diag(diagonal)
    margin = 0.5 * (margin + margin.T)
    return (margin, noise_key)


def draw_margin(key, part):
    margin, noise_key = margin_parts(key)
    return margin


def draw_leaf_factor(key, part):
    margin, noise_key = margin_parts(key)
    quarter = N // 4
    identity = jnp.eye(quarter, dtype=jnp.float32)
    upper_mask = jnp.arange(quarter)[:, None] <= jnp.arange(quarter)[None, :]
    blocks = []
    for quarter_idx in range(4):
        lo_edge = quarter_idx * quarter
        diag_block = margin[lo_edge:lo_edge + quarter, lo_edge:lo_edge + quarter]
        lower_chol = jnp.linalg.cholesky(diag_block)
        inverse = jax.scipy.linalg.solve_triangular(lower_chol, identity, lower=True)
        noise = jax.random.normal(jax.random.fold_in(noise_key, quarter_idx), (quarter, quarter), jnp.float32)
        perturb = jnp.where(upper_mask, noise, 0.0) * (0.2 / jnp.sqrt(jnp.float32(quarter)))
        blocks.append(inverse.T + perturb)
    return jax.scipy.linalg.block_diag(*blocks)


def setup_inputs(seed: int = 0) -> dict:
    streams_of = jax.random.split(jax.random.key(seed), 3)
    margin = draw_margin(jax.random.fold_in(streams_of[2], 71), 0)
    leaf_factor = draw_leaf_factor(jax.random.fold_in(streams_of[2], 71), 0)
    return {"margin": margin, "leaf_factor": leaf_factor}


def matmul(left, right):
    return jnp.dot(left.astype(jnp.float32), right.astype(jnp.float32), precision=lax.Precision.HIGHEST, preferred_element_type=jnp.float32)

def refine(margin, factor):
    applied = matmul(margin, factor)
    coupling = matmul(factor.T, applied)
    defect = jnp.eye(N, dtype=jnp.float32) - coupling
    squares = jnp.sum(defect * defect)
    return (factor + 0.5 * matmul(factor, defect), squares)

def reference(margin, leaf_factor):
    halves = jnp.arange(N) // (N // 2)
    split_margin = jnp.where(halves[:, None] == halves[None, :], margin, jnp.float32(0.0))
    middle, squares_low = refine(split_margin, leaf_factor)
    factor, squares_top = refine(margin, middle)
    errors = jnp.sqrt(jnp.stack([squares_low, squares_top]) / N)
    return (factor, errors)
```

```python
import jax
import jax.numpy as jnp
from jax import lax
from jax.sharding import PartitionSpec as P


AXES = ("seg", "col")
PREC = lax.Precision.HIGHEST


def mm(a, b):
    return lax.dot_general(
        a, b, (((a.ndim - 1,), (0,)), ((), ())),
        precision=PREC, preferred_element_type=jnp.float32,
    )


def device(z, x, y, c):
    return (z * 4 + x) * 8 + y * 2 + c


COORDS = [(z, x, y, c) for z in range(4) for x in range(4) for y in range(4) for c in range(2)]


def send(value, dest):
    pairs = []
    for coord in COORDS:
        to = dest(*coord)
        if to is not None:
            pairs.append((device(*coord), device(*to)))
    return lax.ppermute(value, AXES, pairs)


def swap_core(value):
    return send(value, lambda z, x, y, c: (z, x, y, 1 - c))


def shift(value, axis, step):
    def dest(z, x, y, c):
        if axis == "x":
            return (z, (x + step) % 4, y, c)
        return (z, x, (y + step) % 4, c)

    return send(value, dest)


def put(buf, value, index):
    index = tuple(index) + (0,) * (buf.ndim - len(index))
    return lax.dynamic_update_slice(buf, value, index)


def ring_pieces(value, axis, idx):
    half = value.shape[0] // 2
    fwd = shift(value, axis, 1)
    bwd = shift(value, axis, -1)
    fwd2 = shift(fwd[:half], axis, 1)
    bwd2 = shift(bwd[half:], axis, -1)
    return [
        (value, idx, 0),
        (fwd, (idx + 3) % 4, 0),
        (bwd, (idx + 1) % 4, 0),
        (fwd2, (idx + 2) % 4, 0),
        (bwd2, (idx + 2) % 4, half),
    ]


def ring_gather(value, axis, idx):
    pieces = ring_pieces(value, axis, idx)
    buf = jnp.broadcast_to(value[None], (4,) + value.shape)
    for piece, where, off in pieces[1:]:
        buf = put(buf, piece[None], (where, off))
    return buf


def ring_panel(chunk, axis, idx):
    cols = chunk.shape[1]
    buf = jnp.broadcast_to(chunk.reshape(2, 1, 96, cols), (2, 4, 96, cols))
    for piece, where, off in ring_pieces(chunk, axis, idx)[1:]:
        halves = piece.shape[0] // 96
        buf = put(buf, piece.reshape(halves, 1, 96, cols), (off // 96, where))
    return buf.reshape(2, 384, cols)


def all_sum(value):
    value = value + swap_core(value)
    for axis in ("x", "y"):
        a = value + shift(value, axis, 1)
        value = a + shift(a, axis, 2)
    a = value + send(value, lambda z, x, y, c: ((z + 1) % 4, x, y, c))
    return a + send(a, lambda z, x, y, c: ((z + 2) % 4, x, y, c))


def body(margin, leaf):
    seg, col = lax.axis_index("seg"), lax.axis_index("col")
    z, x, y, c = seg // 4, seg % 4, col // 2, col % 2
    h, k = z // 2, y // 2
    same = h == k

    lz, ly = leaf, leaf
    for s in (1, 2, 3):
        ly = ly + send(leaf, lambda z, x, y, c: ((z + s) % 4, x, y, c) if z == y else None)
        lz = lz + send(leaf, lambda z, x, y, c: (z, x, (y + s) % 4, c) if z == y else None)
    s_cols = lax.dynamic_slice(margin, (0, 768 * y + 384 * c), (192, 384))
    s_own = ring_gather(s_cols, "x", x).reshape(768, 384)
    s_oth = swap_core(s_own)
    ly_all = ring_gather(ly, "x", x).reshape(768, 384)
    lz_oth = swap_core(lz)
    groups = [[4 * zz + xx for xx in range(4)] for zz in range(4)]
    lz_cols = lax.all_to_all(
        lz.reshape(192, 4, 96).transpose(1, 0, 2), "seg", 0, 0, axis_index_groups=groups
    ).reshape(768, 96)
    lz_cols_oth = swap_core(lz_cols)

    def rows_at(v, half):
        return lax.dynamic_slice(v, (384 * half, 0), (384, v.shape[1]))

    applied = mm(s_own, rows_at(ly_all, c)) + mm(s_oth, rows_at(ly_all, 1 - c))
    first = jnp.where(c == 0, lz_cols, lz_cols_oth)
    second = jnp.where(c == 0, lz_cols_oth, lz_cols)

    def tmm(a, b):
        return lax.dot_general(
            a, b, (((0,), (0,)), ((), ())), precision=PREC, preferred_element_type=jnp.float32
        )

    tile = jnp.concatenate([tmm(first, applied), tmm(second, applied)], 0)
    t = jnp.arange(192, dtype=jnp.int32)
    row_ids = 768 * z + 384 * (t // 96) + 96 * x + t % 96
    col_ids = 768 * y + 384 * c + jnp.arange(384, dtype=jnp.int32)
    identity = (row_ids[:, None] == col_ids[None, :]).astype(jnp.float32)
    low = jnp.where(same, identity - tile, 0.0)
    sq_low = jnp.sum(low * low)

    b_own = ring_gather(tile, "y", y)
    b_oth = swap_core(b_own)
    y_tile = 1.5 * identity - 0.5 * tile
    near = send(y_tile, lambda z, x, y, c: (z ^ 1, x, y, c) if z // 2 == y // 2 else None)
    far = send(y_tile, lambda z, x, y, c: (3 - z, x, y, c) if z // 2 == y // 2 else None)
    far2 = send(far, lambda z, x, y, c: (z ^ 1, x, y, c) if z // 2 != y // 2 else None)
    chunk0 = jnp.where(same, y_tile, far)
    chunk1 = near + far2
    q0 = jnp.where(same, z, 3 - z) % 2
    y_pan0 = ring_panel(chunk0, "x", x)
    y_pan1 = ring_panel(chunk1, "x", x)

    def at(v, i):
        return lax.dynamic_index_in_dim(v, i, 0, keepdims=False)

    def times_panels(own, oth, base, pan0, pan1, first_q):
        total = None
        for pan, q in ((pan0, first_q), (pan1, 1 - first_q)):
            for left, half in ((own, c), (oth, 1 - c)):
                part = mm(at(left, base + q), at(pan, half))
                total = part if total is None else total + part
        return total

    u = times_panels(b_own, b_oth, 2 * k, y_pan0, y_pan1, q0)

    u_pan0 = ring_panel(u, "x", x)
    u_near = send(u, lambda z, x, y, c: (z ^ 1, x, y, c))
    u_pan1 = ring_panel(u_near, "x", x)
    q_pan = 1.5 * y_pan0 - 0.5 * u_pan0

    def leaf_times(pan):
        return mm(lz, at(pan, c)) + mm(lz_oth, at(pan, 1 - c))

    g = leaf_times(q_pan)
    mid = jnp.where(same, leaf_times(y_pan0), 0.0)
    g_near = send(g, lambda z, x, y, c: (z, x, y ^ 1, c) if z // 2 == y // 2 else None)
    g_far = send(g, lambda z, x, y, c: (z, x, 3 - y, c) if z // 2 == y // 2 else None)
    g_far2 = send(g_far, lambda z, x, y, c: (z, x, y ^ 1, c) if z // 2 != y // 2 else None)
    g0 = jnp.where(same, g, g_far)
    g1 = g_near + g_far2
    p0 = jnp.where(same, y, 3 - y) % 2
    g_flip = p0 == z % 2
    g_own = jnp.stack([jnp.where(g_flip, g0, g1), jnp.where(g_flip, g1, g0)])
    g_oth = swap_core(g_own)

    zi = z % 2
    coupling = 1.5 * u - 0.5 * times_panels(b_own, b_oth, 2 * h, u_pan0, u_pan1, zi)
    top = identity - coupling
    sq_top = jnp.sum(top * top)
    update = None
    for i, pan in ((0, u_pan0), (1, u_pan1)):
        for left, half in ((g_own, c), (g_oth, 1 - c)):
            part = mm(left[i], at(pan, half))
            update = part if update is None else update + part
    factor = 1.5 * mid - 0.5 * update

    lane = lax.broadcasted_iota(jnp.int32, (8, 128), 1)
    sums = all_sum(jnp.where(lane == 0, sq_low, jnp.where(lane == 1, sq_top, 0.0)))
    errors = jnp.sqrt(sums[0, :2] / 3072)
    return factor, errors


def solution(mesh):
    return jax.shard_map(
        body,
        mesh=mesh,
        in_specs=(P("seg", None), P("seg", "col")),
        out_specs=(P("seg", "col"), P()),
        check_vma=False,
    )
```

```python
import jax
import jax.numpy as jnp
from jax import lax
from jax.sharding import PartitionSpec as P


AXES = ("seg", "col")
PREC = lax.Precision.HIGHEST


def mm(a, b):
    return lax.dot_general(
        a, b, (((a.ndim - 1,), (0,)), ((), ())),
        precision=PREC, preferred_element_type=jnp.float32,
    )


def device(z, x, y, c):
    return (z * 4 + x) * 8 + y * 2 + c


COORDS = [(z, x, y, c) for z in range(4) for x in range(4) for y in range(4) for c in range(2)]


def send(value, dest):
    pairs = []
    for coord in COORDS:
        to = dest(*coord)
        if to is not None:
            pairs.append((device(*coord), device(*to)))
    return lax.ppermute(value, AXES, pairs)


def swap_core(value):
    return send(value, lambda z, x, y, c: (z, x, y, 1 - c))


def shift(value, axis, step):
    def dest(z, x, y, c):
        if axis == "x":
            return (z, (x + step) % 4, y, c)
        return (z, x, (y + step) % 4, c)

    return send(value, dest)


def put(buf, value, index):
    index = tuple(index) + (0,) * (buf.ndim - len(index))
    return lax.dynamic_update_slice(buf, value, index)


def ring_pieces(value, axis, idx):
    half = value.shape[0] // 2
    fwd = shift(value, axis, 1)
    bwd = shift(value, axis, -1)
    fwd2 = shift(fwd[:half], axis, 1)
    bwd2 = shift(bwd[half:], axis, -1)
    return [
        (value, idx, 0),
        (fwd, (idx + 3) % 4, 0),
        (bwd, (idx + 1) % 4, 0),
        (fwd2, (idx + 2) % 4, 0),
        (bwd2, (idx + 2) % 4, half),
    ]


def ring_gather(value, axis, idx):
    pieces = ring_pieces(value, axis, idx)
    buf = jnp.broadcast_to(value[None], (4,) + value.shape)
    for piece, where, off in pieces[1:]:
        buf = put(buf, piece[None], (where, off))
    return buf


def all_sum(value):
    for axis, n in (("seg", 16), ("col", 8)):
        parts = lax.all_to_all(jnp.broadcast_to(value, (n, 128)), axis, 0, 0, tiled=True)
        value = jnp.sum(parts, 0, keepdims=True)
    return value


def spread_z(value):
    one = send(value, lambda z, x, y, c: ((z + 1) % 4, x, y, c) if z == y else None)
    value = value + one

    def dest(z, x, y, c):
        if z == y:
            return ((z + 3) % 4, x, y, c)
        return ((z + 1) % 4, x, y, c) if z == (y + 1) % 4 else None

    return value + send(value, dest)


def spread_y(value):
    one = send(value, lambda z, x, y, c: (z, x, (y + 1) % 4, c) if z == y else None)
    value = value + one

    def dest(z, x, y, c):
        if z == y:
            return (z, x, (y + 3) % 4, c)
        return (z, x, (y + 1) % 4, c) if y == (z + 1) % 4 else None

    return value + send(value, dest)


def body(margin, leaf):
    seg, col = lax.axis_index("seg"), lax.axis_index("col")
    z, x, y, c = seg // 4, seg % 4, col // 2, col % 2
    h, k = z // 2, y // 2
    same = h == k

    ly = spread_z(leaf)
    lz = spread_y(leaf)
    s_cols = lax.dynamic_slice(margin, (0, 768 * y + 384 * c), (192, 384))
    s_own = ring_gather(s_cols, "x", x).reshape(768, 384)
    s_oth = swap_core(s_own)
    ly_all = ring_gather(ly, "x", x).reshape(768, 384)
    lz_oth = swap_core(lz)

    def my_cols(where):
        return jnp.where(where % 2 == 0, lz[:, :192], lz[:, 192:])

    lz_cols = jnp.broadcast_to(my_cols(x)[None], (4, 192, 192))
    for s in (1, 3, 2):
        piece = send(
            my_cols((x + s) % 4),
            lambda z, x, y, c: (z, (x + s) % 4, y, c) if c == (x + s) % 4 // 2 else None,
        )
        lz_cols = put(lz_cols, piece[None], ((x - s) % 4,))
    lz_cols = jnp.where(c == x // 2, lz_cols, swap_core(lz_cols)).reshape(768, 192)

    def rows_at(v, half):
        return lax.dynamic_slice(v, (384 * half, 0), (384, v.shape[1]))

    applied = mm(s_own, rows_at(ly_all, c)) + mm(s_oth, rows_at(ly_all, 1 - c))
    tile = lax.dot_general(
        lz_cols, applied, (((0,), (0,)), ((), ())), precision=PREC, preferred_element_type=jnp.float32
    )
    row_ids = 192 * seg + jnp.arange(192, dtype=jnp.int32)
    col_ids = 384 * col + jnp.arange(384, dtype=jnp.int32)
    identity = (row_ids[:, None] == col_ids[None, :]).astype(jnp.float32)
    low = jnp.where(same, identity - tile, 0.0)
    sq_low = jnp.sum(low * low)

    def panel(chunk):
        return ring_gather(chunk, "x", x).reshape(2, 384, 384)

    y_tile = 1.5 * identity - 0.5 * tile
    far = send(y_tile, lambda z, x, y, c: (3 - z, x, y, c) if z // 2 == y // 2 else None)
    chunk0 = jnp.where(same, y_tile, far)
    chunk1 = send(chunk0, lambda z, x, y, c: (z ^ 1, x, y, c))
    q0 = jnp.where(same, z, 3 - z) % 2
    y_pan0 = panel(chunk0)
    y_pan1 = panel(chunk1)
    b_near = send(tile, lambda z, x, y, c: (z, x, y ^ 1, c))
    b_far = send(tile, lambda z, x, y, c: (z, x, 3 - y, c))
    b_far2 = send(b_far, lambda z, x, y, c: (z, x, y ^ 1, c))
    yi, zi = y % 2, z % 2
    pair = jnp.stack([tile, b_near])
    pair_oth = swap_core(pair)
    pair_h = jnp.where(same, pair, jnp.stack([b_far, b_far2]))
    pair_h_oth = swap_core(pair_h)
    p0 = jnp.where(same, y, 3 - y) % 2

    def at(v, i):
        return lax.dynamic_index_in_dim(v, i, 0, keepdims=False)

    def times_panels(own, oth, first_p, pan0, pan1, first_q):
        flip = (first_p + first_q) % 2
        total = None
        for i, pan in ((0, pan0), (1, pan1)):
            for left, half in ((own, c), (oth, 1 - c)):
                part = mm(at(left, (i + flip) % 2), at(pan, half))
                total = part if total is None else total + part
        return total

    u = times_panels(pair, pair_oth, yi, y_pan0, y_pan1, q0)

    u_pan0 = panel(u)
    u_near = send(u, lambda z, x, y, c: (z ^ 1, x, y, c))
    u_pan1 = panel(u_near)
    q_pan = 1.5 * y_pan0 - 0.5 * u_pan0

    def leaf_times(pan):
        return mm(lz, at(pan, c)) + mm(lz_oth, at(pan, 1 - c))

    g = leaf_times(q_pan)
    mid = jnp.where(same, leaf_times(y_pan0), 0.0)
    g_far = send(g, lambda z, x, y, c: (z, x, 3 - y, c) if z // 2 == y // 2 else None)
    g0 = jnp.where(same, g, g_far)
    g1 = send(g0, lambda z, x, y, c: (z, x, y ^ 1, c))
    g_own = jnp.stack([g0, g1])
    g_oth = swap_core(g_own)

    coupling = 1.5 * u - 0.5 * times_panels(pair_h, pair_h_oth, p0, u_pan0, u_pan1, zi)
    top = identity - coupling
    sq_top = jnp.sum(top * top)
    factor = 1.5 * mid - 0.5 * times_panels(g_own, g_oth, p0, u_pan0, u_pan1, zi)

    lane = lax.broadcasted_iota(jnp.int32, (1, 128), 1)
    sums = all_sum(jnp.where(lane == 0, sq_low, jnp.where(lane == 1, sq_top, 0.0)))
    errors = jnp.sqrt(sums[0, :2] / 3072)
    return factor, errors


def solution(mesh):
    return jax.shard_map(
        body,
        mesh=mesh,
        in_specs=(P("seg", None), P("seg", "col")),
        out_specs=(P("seg", "col"), P()),
        check_vma=False,
    )
```

```python
import jax
import jax.numpy as jnp
from jax import lax
from jax.sharding import PartitionSpec as P


AXES = ("seg", "col")
FULL, THREE = lax.Precision.HIGHEST, lax.Precision.HIGH

GRAY = (0, 1, 1, 0)


def mm(a, b, left_dim=1, precision=THREE):
    return lax.dot_general(
        a, b, (((left_dim,), (0,)), ((), ())),
        precision=precision, preferred_element_type=jnp.float32,
    )


def device(z, x, y, c):
    return (z * 4 + x) * 8 + y * 2 + c


COORDS = [(z, x, y, c) for z in range(4) for x in range(4) for y in range(4) for c in range(2)]


def send(value, dest):
    pairs = []
    for coord in COORDS:
        to = dest(*coord)
        if to is not None:
            pairs.append((device(*coord), device(*to)))
    return lax.ppermute(value, AXES, pairs)


def filled(x, c):
    return x < 2 or c == 1


def swap_core(value):
    return send(value, lambda z, x, y, c: (z, x, y, 1 - c))


def swap_row_half(value):
    return send(value, lambda z, x, y, c: (z, 3 - x, y, c))


def swap_col_half(value):
    return send(value, lambda z, x, y, c: (z, x ^ 1, y, c))


def put(buf, value, index):
    index = tuple(index) + (0,) * (buf.ndim - len(index))
    return lax.dynamic_update_slice(buf, value, index)


def ring_gather(value, idx):
    half = value.shape[0] // 2
    fwd = send(value, lambda z, x, y, c: (z, (x + 1) % 4, y, c))
    bwd = send(value, lambda z, x, y, c: (z, (x + 3) % 4, y, c))
    fwd2 = send(fwd[:half], lambda z, x, y, c: (z, (x + 1) % 4, y, c))
    bwd2 = send(bwd[half:], lambda z, x, y, c: (z, (x + 3) % 4, y, c))
    buf = jnp.broadcast_to(value[None], (4,) + value.shape)
    buf = put(buf, fwd[None], ((idx + 3) % 4,))
    buf = put(buf, bwd[None], ((idx + 1) % 4,))
    buf = put(buf, fwd2[None], ((idx + 2) % 4, 0))
    return put(buf, bwd2[None], ((idx + 2) % 4, half))


def all_sum(value):
    for axis, n in (("seg", 16), ("col", 8)):
        parts = lax.all_to_all(jnp.broadcast_to(value, (n, 128)), axis, 0, 0, tiled=True)
        value = jnp.sum(parts, 0, keepdims=True)
    return value


def compute(margin, leaf):
    seg, col = lax.axis_index("seg"), lax.axis_index("col")
    z, x, y, c = seg // 4, seg % 4, col // 2, col % 2
    xr, xc = x // 2, (x + 1) // 2 % 2
    yi, zi = y % 2, z % 2
    same = z // 2 == y // 2

    ly, lz = leaf, lax.optimization_barrier(leaf)
    for s in (1, 3, 2):
        ly = ly + send(leaf, lambda z, x, y, c: ((z + s) % 4, x, y, c) if z == y and filled(x, c) else None)
        lz = lz + send(leaf, lambda z, x, y, c: (z, x, (y + s) % 4, c) if z == y and filled(x, c) else None)
    s_cols = lax.dynamic_slice(margin, (0, 768 * y + 384 * c), (192, 384))
    s_rows = ring_gather(s_cols, x).reshape(768, 384)

    def leaf_rows(value, chips):
        def dest(first):
            def fn(z, x, y, c):
                return (z, chips[c][(x + first) % 2], y, x // 2) if filled(x, c) else None

            return fn

        one, two = (send(value, dest(i)) for i in (0, 1))
        return one, two

    ly_a, ly_b = leaf_rows(ly, ((0, 3), (1, 2)))
    lz_a, lz_b = leaf_rows(lz, ((0, 1), (2, 3)))
    ly_half = jnp.concatenate([jnp.where(xr == 0, ly_a, ly_b), jnp.where(xr == 0, ly_b, ly_a)])
    even = x % 2 == 0
    lz_half = jnp.concatenate([jnp.where(even, lz_a, lz_b), jnp.where(even, lz_b, lz_a)])
    lz_pair = swap_col_half(lz)
    mine = c == x % 2
    lz_own = jnp.where(mine, lz, lz_pair)
    lz_oth = swap_core(jnp.where(mine, lz_pair, lz))

    def rows_at(v, start, size):
        return lax.dynamic_slice(v, (start, 0), (size, v.shape[1]))

    applied = mm(s_rows, ly_half)
    applied = rows_at(applied, 384 * c, 384) + swap_core(rows_at(applied, 384 * (1 - c), 384))
    tile = mm(lz_half, applied, 0)
    tile = rows_at(tile, 192 * c, 192) + swap_core(rows_at(tile, 192 * (1 - c), 192))
    row_ids = 768 * z + 384 * xr + 192 * c + jnp.arange(192, dtype=jnp.int32)
    col_ids = 768 * y + 384 * xc + jnp.arange(384, dtype=jnp.int32)
    identity = (row_ids[:, None] == col_ids[None, :]).astype(jnp.float32)
    low = jnp.where(same, identity - lax.optimization_barrier(tile), 0.0)
    sq_low = jnp.sum(low * low)

    def panel(own, near):
        over = swap_row_half(own)
        cross = swap_row_half(near)
        first = (own, swap_core(own), over, swap_core(over))
        last = (near, swap_core(near), cross, swap_core(cross))

        def fill(tiles):
            buf = jnp.broadcast_to(tiles[0], (2, 2, 192, 384))
            for n in (1, 2, 3):
                buf = put(buf, tiles[n][None, None], (n // 2, c if n == 2 else 1 - c))
            return buf

        half = fill(first)
        both = jnp.concatenate([half[None], jnp.broadcast_to(near, (1, 2, 2, 192, 384))])
        for n in (1, 2, 3):
            both = put(both, last[n][None, None, None], (1, n // 2, c if n == 2 else 1 - c))
        return half.reshape(1, 2, 384, 384), both.reshape(2, 2, 384, 384)

    def block(pan, i, b):
        pan = pan.reshape(pan.shape[0] * 2, 384, 384)
        return lax.dynamic_index_in_dim(pan, 2 * i + b, 0, keepdims=False)

    def times_panel(left, flip, pan, precision=THREE):
        total = None
        odd = x % 2
        for j in (0, 1):
            for l in (0, 1):
                part = mm(left[j][l], block(pan, j ^ flip, l ^ odd), 1, precision)
                total = part if total is None else total + part
        return total

    y_tile = 1.5 * identity - 0.5 * tile
    y_far = send(y_tile, lambda z, x, y, c: (3 - z, x, y, c) if z // 2 == y // 2 else None)
    y0 = jnp.where(same, y_tile, y_far)
    y1 = send(y0, lambda z, x, y, c: (z ^ 1, x, y, c))
    q0 = jnp.where(same, z, 3 - z) % 2
    y_own, y_pan = panel(y0, y1)
    b_near = send(tile, lambda z, x, y, c: (z, x, y ^ 1, c))
    b_cross = swap_col_half(b_near)
    left = ((tile, swap_col_half(tile)), (b_near, b_cross))
    tiles = lax.optimization_barrier(jnp.stack([left[j][l] for j in (0, 1) for l in (0, 1)]))
    u = times_panel(tiles.reshape(2, 2, 192, 384), yi ^ q0, y_pan, FULL)

    b_far = send(tile, lambda z, x, y, c: (z, x, 3 - y, c))
    b_far2 = send(b_far, lambda z, x, y, c: (z, x, y ^ 1, c))
    far_cross = swap_col_half(b_far2)
    far = ((b_far, swap_col_half(b_far)), (b_far2, far_cross))
    rows = jnp.stack([jnp.where(same, left[j][l], far[j][l]) for j in (0, 1) for l in (0, 1)])
    rows = lax.optimization_barrier(rows).reshape(2, 2, 192, 384)
    p0 = jnp.where(same, y, 3 - y) % 2

    u_near = send(u, lambda z, x, y, c: (z ^ 1, x, y, c))
    u_own, u_pan = panel(u, u_near)

    def leaf_times(pan):
        own = mm(lz_own, block(pan, 0, c ^ xr), 1, FULL)
        return own + mm(lz_oth, block(pan, 0, 1 ^ c ^ xr), 1, FULL)

    q_pan = 1.5 * y_own - 0.5 * u_own
    g = leaf_times(q_pan)
    mid = lax.optimization_barrier(jnp.where(same, leaf_times(y_own), 0.0))
    g_far = send(g, lambda z, x, y, c: (z, x, 3 - y, c) if z // 2 == y // 2 else None)
    g0 = jnp.where(same, g, g_far)
    g1 = send(g0, lambda z, x, y, c: (z, x, y ^ 1, c))
    g_cross = swap_col_half(g1)
    g_rows = ((g0, swap_col_half(g0)), (g1, g_cross))

    coupling = 1.5 * u - 0.5 * times_panel(rows, p0 ^ zi, u_pan)
    top = identity - coupling
    sq_top = jnp.sum(top * top)
    factor = 1.5 * mid - 0.5 * times_panel(g_rows, p0 ^ zi, u_pan)
    factor = send(factor, lambda z, x, y, c: (z, x // 2 * 2 + c, y, GRAY[x]))

    lane = lax.broadcasted_iota(jnp.int32, (1, 128), 1)
    sums = all_sum(jnp.where(lane == 0, sq_low, jnp.where(lane == 1, sq_top, 0.0)))
    errors = jnp.sqrt(sums[0, :2] / 3072)
    return factor, errors


def solution(mesh):
    return jax.shard_map(
        compute,
        mesh=mesh,
        in_specs=(P("seg", None), P("seg", "col")),
        out_specs=(P("seg", "col"), P()),
        check_vma=False,
    )
```

```python
import jax
import jax.numpy as jnp
from jax import lax
from jax.sharding import PartitionSpec as P


AXES = ("seg", "col")
PREC = lax.Precision.HIGHEST

GRAY = (0, 1, 1, 0)


def mm(a, b, left_dim=1):
    return lax.dot_general(
        a, b, (((left_dim,), (0,)), ((), ())),
        precision=PREC, preferred_element_type=jnp.float32,
    )


def device(z, x, y, c):
    return (z * 4 + x) * 8 + y * 2 + c


COORDS = [(z, x, y, c) for z in range(4) for x in range(4) for y in range(4) for c in range(2)]


def send(value, dest):
    pairs = []
    for coord in COORDS:
        to = dest(*coord)
        if to is not None:
            pairs.append((device(*coord), device(*to)))
    return lax.ppermute(value, AXES, pairs)


def filled(x, c):
    return x < 2 or c == 1


def swap_core(value):
    return send(value, lambda z, x, y, c: (z, x, y, 1 - c))


def swap_row_half(value):
    return send(value, lambda z, x, y, c: (z, 3 - x, y, c))


def swap_col_half(value):
    return send(value, lambda z, x, y, c: (z, x ^ 1, y, c))


def put(buf, value, index):
    index = tuple(index) + (0,) * (buf.ndim - len(index))
    return lax.dynamic_update_slice(buf, value, index)


def ring_gather(value, idx):
    half = value.shape[0] // 2
    fwd = send(value, lambda z, x, y, c: (z, (x + 1) % 4, y, c))
    bwd = send(value, lambda z, x, y, c: (z, (x + 3) % 4, y, c))
    fwd2 = send(fwd[:half], lambda z, x, y, c: (z, (x + 1) % 4, y, c))
    bwd2 = send(bwd[half:], lambda z, x, y, c: (z, (x + 3) % 4, y, c))
    buf = jnp.broadcast_to(value[None], (4,) + value.shape)
    buf = put(buf, fwd[None], ((idx + 3) % 4,))
    buf = put(buf, bwd[None], ((idx + 1) % 4,))
    buf = put(buf, fwd2[None], ((idx + 2) % 4, 0))
    return put(buf, bwd2[None], ((idx + 2) % 4, half))


def all_sum(value):
    for axis, n in (("seg", 16), ("col", 8)):
        parts = lax.all_to_all(jnp.broadcast_to(value, (n, 128)), axis, 0, 0, tiled=True)
        value = jnp.sum(parts, 0, keepdims=True)
    return value


def compute(margin, leaf):
    seg, col = lax.axis_index("seg"), lax.axis_index("col")
    z, x, y, c = seg // 4, seg % 4, col // 2, col % 2
    xr, xc = x // 2, (x + 1) // 2 % 2
    yi, zi = y % 2, z % 2
    same = z // 2 == y // 2

    ly, lz = leaf, lax.optimization_barrier(leaf)
    for s in (1, 3, 2):
        ly = ly + send(leaf, lambda z, x, y, c: ((z + s) % 4, x, y, c) if z == y and filled(x, c) else None)
        lz = lz + send(leaf, lambda z, x, y, c: (z, x, (y + s) % 4, c) if z == y and filled(x, c) else None)
    s_cols = lax.dynamic_slice(margin, (0, 768 * y + 384 * c), (192, 384))
    s_rows = ring_gather(s_cols, x).reshape(768, 384)

    def leaf_rows(value, chips):
        def dest(first):
            def fn(z, x, y, c):
                return (z, chips[c][(x + first) % 2], y, x // 2) if filled(x, c) else None

            return fn

        one, two = (send(value, dest(i)) for i in (0, 1))
        return one, two

    ly_a, ly_b = leaf_rows(ly, ((0, 3), (1, 2)))
    lz_a, lz_b = leaf_rows(lz, ((0, 1), (2, 3)))
    ly_half = jnp.concatenate([jnp.where(xr == 0, ly_a, ly_b), jnp.where(xr == 0, ly_b, ly_a)])
    even = x % 2 == 0
    lz_half = jnp.concatenate([jnp.where(even, lz_a, lz_b), jnp.where(even, lz_b, lz_a)])
    lz_pair = swap_col_half(lz)
    mine = c == x % 2
    lz_own = jnp.where(mine, lz, lz_pair)
    lz_oth = swap_core(jnp.where(mine, lz_pair, lz))

    def rows_at(v, start, size):
        return lax.dynamic_slice(v, (start, 0), (size, v.shape[1]))

    applied = mm(s_rows, ly_half)
    applied = rows_at(applied, 384 * c, 384) + swap_core(rows_at(applied, 384 * (1 - c), 384))
    tile = mm(lz_half, applied, 0)
    tile = rows_at(tile, 192 * c, 192) + swap_core(rows_at(tile, 192 * (1 - c), 192))
    row_ids = 768 * z + 384 * xr + 192 * c + jnp.arange(192, dtype=jnp.int32)
    col_ids = 768 * y + 384 * xc + jnp.arange(384, dtype=jnp.int32)
    identity = (row_ids[:, None] == col_ids[None, :]).astype(jnp.float32)
    low = jnp.where(same, identity - lax.optimization_barrier(tile), 0.0)
    sq_low = jnp.sum(low * low)

    def panel(own, near):
        over = swap_row_half(own)
        cross = swap_row_half(near)
        first = (own, swap_core(own), over, swap_core(over))
        last = (near, swap_core(near), cross, swap_core(cross))

        def fill(tiles):
            buf = jnp.broadcast_to(tiles[0], (2, 2, 192, 384))
            for n in (1, 2, 3):
                buf = put(buf, tiles[n][None, None], (n // 2, c if n == 2 else 1 - c))
            return buf

        half = fill(first)
        both = jnp.concatenate([half[None], jnp.broadcast_to(near, (1, 2, 2, 192, 384))])
        for n in (1, 2, 3):
            both = put(both, last[n][None, None, None], (1, n // 2, c if n == 2 else 1 - c))
        return half.reshape(1, 2, 384, 384), both.reshape(2, 2, 384, 384)

    def block(pan, i, b):
        pan = pan.reshape(pan.shape[0] * 2, 384, 384)
        return lax.dynamic_index_in_dim(pan, 2 * i + b, 0, keepdims=False)

    def times_panel(left, flip, pan):
        total = None
        odd = x % 2
        for j in (0, 1):
            for l in (0, 1):
                part = mm(left[j][l], block(pan, j ^ flip, l ^ odd))
                total = part if total is None else total + part
        return total

    y_tile = 1.5 * identity - 0.5 * tile
    y_far = send(y_tile, lambda z, x, y, c: (3 - z, x, y, c) if z // 2 == y // 2 else None)
    y0 = jnp.where(same, y_tile, y_far)
    y1 = send(y0, lambda z, x, y, c: (z ^ 1, x, y, c))
    q0 = jnp.where(same, z, 3 - z) % 2
    y_own, y_pan = panel(y0, y1)
    b_near = send(tile, lambda z, x, y, c: (z, x, y ^ 1, c))
    b_cross = swap_col_half(b_near)
    left = ((tile, swap_col_half(tile)), (b_near, b_cross))
    tiles = lax.optimization_barrier(jnp.stack([left[j][l] for j in (0, 1) for l in (0, 1)]))
    u = times_panel(tiles.reshape(2, 2, 192, 384), yi ^ q0, y_pan)

    b_far = send(tile, lambda z, x, y, c: (z, x, 3 - y, c))
    b_far2 = send(b_far, lambda z, x, y, c: (z, x, y ^ 1, c))
    far_cross = swap_col_half(b_far2)
    far = ((b_far, swap_col_half(b_far)), (b_far2, far_cross))
    rows = jnp.stack([jnp.where(same, left[j][l], far[j][l]) for j in (0, 1) for l in (0, 1)])
    rows = lax.optimization_barrier(rows).reshape(2, 2, 192, 384)
    p0 = jnp.where(same, y, 3 - y) % 2

    u_near = send(u, lambda z, x, y, c: (z ^ 1, x, y, c))
    u_own, u_pan = panel(u, u_near)

    def leaf_times(pan):
        return mm(lz_own, block(pan, 0, c ^ xr)) + mm(lz_oth, block(pan, 0, 1 ^ c ^ xr))

    q_pan = 1.5 * y_own - 0.5 * u_own
    g = leaf_times(q_pan)
    mid = lax.optimization_barrier(jnp.where(same, leaf_times(y_own), 0.0))
    g_far = send(g, lambda z, x, y, c: (z, x, 3 - y, c) if z // 2 == y // 2 else None)
    g0 = jnp.where(same, g, g_far)
    g1 = send(g0, lambda z, x, y, c: (z, x, y ^ 1, c))
    g_cross = swap_col_half(g1)
    g_rows = ((g0, swap_col_half(g0)), (g1, g_cross))

    coupling = 1.5 * u - 0.5 * times_panel(rows, p0 ^ zi, u_pan)
    top = identity - coupling
    sq_top = jnp.sum(top * top)
    factor = 1.5 * mid - 0.5 * times_panel(g_rows, p0 ^ zi, u_pan)
    factor = send(factor, lambda z, x, y, c: (z, x // 2 * 2 + c, y, GRAY[x]))

    lane = lax.broadcasted_iota(jnp.int32, (1, 128), 1)
    sums = all_sum(jnp.where(lane == 0, sq_low, jnp.where(lane == 1, sq_top, 0.0)))
    errors = jnp.sqrt(sums[0, :2] / 3072)
    return factor, errors


def solution(mesh):
    return jax.shard_map(
        compute,
        mesh=mesh,
        in_specs=(P("seg", None), P("seg", "col")),
        out_specs=(P("seg", "col"), P()),
        check_vma=False,
    )
```
